32 devices in a mesh: ep: 8 (over z, y), tp: 4 (over x, core).
Axes of the slice: x: 2, y: 2, z: 4, core: 2. Of those that a mesh axis runs over, the one named last changes fastest.
Arguments:
- tokens: bfloat16 [1024, 3584], P('ep', 'tp'), may hold values from -6 to 6
- tangents: bfloat16 [2, 1024, 3584], P(None, 'ep', 'tp'), may hold values from -6 to 6
- tangent_mask: int32 [2, 1024, 28], P(None, 'ep', 'tp'), may hold values 0 or 1
- expert_ids: int32 [1024, 2], P('ep'), may hold values from 0 to 7, all different within a row; in each aligned block of 128 rows (0 to 127, 128 to 255, ...) at most 48 rows name the same one
- gate_fixed: int32 [1024, 2], P('ep'), may hold values from 4096 to 65535
- w_up: bfloat16 [8, 3584, 1024], P('ep', None, 'tp'), may hold values from -0.09375 to 0.09375
- w_down: bfloat16 [8, 1024, 3584], P('ep', None, 'tp'), may hold values from -0.1875 to 0.1875
Outputs:
- mixed: bfloat16 [1024, 3584], P('ep', 'tp')
- mixed_tangents: bfloat16 [2, 1024, 3584], P(None, 'ep', 'tp')
The draws below stay inside these ranges and needn't reach their ends.
Inputs may be any that keep to these rules, and one draw needn't show every extreme that they name: `expert_ids`: each row names 2 different experts; among the rows of the tokens of one index of ep (128 aligned rows) no expert is named by more than 48 rows, a bound that some block reaches.
All inputs are finite; a program needn't handle non-finite values. No bound on the sum of `tangent_mask` on one device may be relied on, other than what follows from the above.
Results may differ from the reference program's by a relative error of at most 0.008.
Values may be sent and summed in bfloat16 or wider, within the bound.
A program may use at most 64 MiB of HBM per device.

```python
import math
import jax
import jax.numpy as jnp
import numpy as np
from jax import lax

D = 3584
FF = 1024
TOP = 2
TOK_DEV = 128
EXPERTS = 8
CAP = 48
TOKENS = 1024
DB = 28
N_EP = 8


def touch_ends(entries, key, smallest, largest):
    index_at = [jax.random.randint(jax.random.fold_in(key, axis), (), 0, length) for axis, length in enumerate(entries.shape)]
    widest = entries.shape.index(max(entries.shape))
    neighbour = index_at[:widest] + [(index_at[widest] + 1) % entries.shape[widest]] + index_at[widest + 1:]
    return entries.at[tuple(index_at)].set(smallest).at[tuple(neighbour)].set(largest)


def block_levels(key, shape, cuts, least, largest):
    gain, own = 1.0, jax.random.fold_in(key, 6)
    for axis_at, parts in cuts:
        heights = jnp.exp(jax.random.uniform(jax.random.fold_in(own, axis_at), (parts,), jnp.float32, least / len(cuts), largest / len(cuts)))
        gain = gain * jnp.repeat(heights, shape[axis_at] // parts).reshape([-1 if axis == axis_at else 1 for axis in range(len(shape))])
    return gain


def deal_out(rng, own, number, rows, count, top, reach, skew):
    sequence = jax.random.permutation(rng, count)
    crowded, usual = portions_of(count, rows * top, reach, skew, True), portions_of(count, rows * top, reach, skew, False)
    places = jnp.arange(count)

    def named(lengths, turn):
        used = int((lengths > 0).sum())
        fixed = max(1, used // 4)
        moved = fixed + (places - fixed + turn * (used - fixed)) % max(1, count - fixed)
        return jnp.zeros((count,), jnp.int32).at[sequence[jnp.where(places < fixed, places, moved)]].set(jnp.asarray(lengths, jnp.int32))

    lengths = jnp.where(number % 4 == 0, named(crowded, number // 4), named(usual, number - number // 4 - 1))
    mixed = jax.random.permutation(jax.random.fold_in(own, 3), count)
    giver, taker = mixed[0:count // 2 * 2:2], mixed[1:count // 2 * 2:2]
    margin = jnp.minimum(lengths[giver] - 1, reach - lengths[taker]) // 2
    margin = jnp.where((giver == sequence[0]) | (taker == sequence[0]) | (lengths[taker] == 0), 0, jnp.maximum(margin, 0))
    moved = jax.random.randint(jax.random.fold_in(own, 4), (count // 2,), 0, 1 << 20) % (margin + 1)
    lengths = lengths.at[giver].add(-moved).at[taker].add(moved)
    labels = jnp.searchsorted(jnp.cumsum(lengths), jnp.arange(rows * top), side="right").astype(jnp.int32)
    table = labels.reshape(top, rows).T
    table = table[jax.random.permutation(jax.random.fold_in(own, 1), rows)]
    turn = jax.random.randint(jax.random.fold_in(own, 2), (rows, 1), 0, top)
    return jnp.take_along_axis(table, (jnp.arange(top)[None, :] + turn) % top, axis=1)


def portions_of(count, total, reach, skew, full):
    loads = [(1 << 20) // math.isqrt(grade ** skew) + 1 for grade in range(1, count + 1)]
    largest = reach if full else min(reach, max(-(-total // count), total * loads[0] // sum(loads)))
    least = 1 if total - largest >= count - 1 else 0
    counts, surplus = [largest] + [least] * (count - 1), total - largest - least * (count - 1)
    while surplus > 0:
        free = [i for i in range(1, count) if counts[i] < largest] or [i for i in range(1, count) if counts[i] < reach]
        whole, left = sum([loads[i] for i in free]), surplus
        for i in free:
            addition = min(reach - counts[i], max(1, left * loads[i] // whole), surplus)
            counts[i] = counts[i] + addition
            surplus = surplus - addition
    return np.array(counts)


def scatter_about(stream_key, dims, spread, reach, shards=(), kind=jnp.bfloat16):
    loudness = block_levels(stream_key, dims, shards, -0.22, 0.18) if shards else 1.0
    values = jax.random.normal(stream_key, dims, jnp.float32) * spread * loudness
    return jnp.minimum(jnp.maximum(values, -reach), reach).astype(kind)


def setup_inputs(seed: int = 0) -> dict:
    streams_of = jax.random.split(jax.random.key(seed), 8)
    tokens = scatter_about(streams_of[0], (TOKENS, D), 1.0, 6.0, ((0, 8), (1, 4)))
    tangents = scatter_about(streams_of[1], (2, TOKENS, D), 1.0, 6.0, ((1, 8), (2, 4)))
    tangent_mask = touch_ends((jax.random.randint(streams_of[2], (2, TOKENS, DB), 0, 2) < 1).astype(jnp.int32), jax.random.fold_in(streams_of[2], 1), 0, 1)
    expert_ids_keys = jax.random.split(jax.random.fold_in(streams_of[3], 1), TOKENS // TOK_DEV)
    expert_ids_turns = jax.random.permutation(jax.random.fold_in(streams_of[3], 3), TOKENS // TOK_DEV)
    expert_ids = jax.vmap(lambda own, number: deal_out(jax.random.fold_in(streams_of[3], 2), own, number, TOK_DEV, EXPERTS, TOP, CAP, 2))(expert_ids_keys, expert_ids_turns).reshape((TOKENS, TOP))
    gate_fixed = touch_ends(jax.random.randint(streams_of[4], (TOKENS, TOP), 4096, 65536), jax.random.fold_in(streams_of[4], 1), 4096, 65535).astype(jnp.int32)
    w_up = scatter_about(streams_of[5], (EXPERTS, D, FF), D ** -0.5, 0.09375, ((0, 8), (2, 4)))
    w_down = scatter_about(streams_of[6], (EXPERTS, FF, D), FF ** -0.5, 0.1875, ((0, 8), (2, 4)))
    return dict(tokens=tokens, tangents=tangents, tangent_mask=tangent_mask, expert_ids=expert_ids, gate_fixed=gate_fixed, w_up=w_up, w_down=w_down)


def reference(tokens, tangents, tangent_mask, expert_ids, gate_fixed, w_up, w_down):
    total, width = tokens.shape
    blocks = tangent_mask.shape[2]
    keep = tangent_mask.astype(jnp.bfloat16)
    masked = (tangents.reshape(2, total, blocks, width // blocks) * keep[..., None]).reshape(2, total, width)
    stacked = jnp.concatenate([tokens[None], masked], axis=0)
    flat_ids = expert_ids.reshape(-1)
    gates = (gate_fixed.astype(jnp.float32) / 65536.0).reshape(-1)
    pairs = flat_ids.shape[0]
    most = N_EP * CAP

    def one_expert(carry, expert):
        index = jnp.nonzero(flat_ids == expert, size=most, fill_value=pairs)[0].astype(jnp.int32)
        token = (index // TOP).astype(jnp.int32)
        rows = jnp.take(stacked, token, axis=1, mode="fill", fill_value=0)
        weight = jnp.take(gates, index, mode="fill", fill_value=0.0)
        up_mat = lax.dynamic_index_in_dim(w_up, expert, 0, keepdims=False).astype(jnp.float32)
        down_mat = lax.dynamic_index_in_dim(w_down, expert, 0, keepdims=False).astype(jnp.float32)
        hidden = jnp.einsum("tmd,df->tmf", rows.astype(jnp.float32), up_mat)
        base = hidden[0]
        sig = jax.nn.sigmoid(base)
        slope = sig * (1.0 + base * (1.0 - sig))
        acts = jnp.concatenate([(base * sig)[None], slope[None] * hidden[1:]], axis=0).astype(jnp.bfloat16)
        outs = jnp.einsum("tmf,fd->tmd", acts.astype(jnp.float32), down_mat).astype(jnp.bfloat16)
        contrib = outs.astype(jnp.float32) * weight[None, :, None]
        carry = carry.at[:, token].add(contrib, mode="drop")
        return carry, None

    start = jnp.zeros((3, total, width), jnp.float32)
    final, _ = lax.scan(one_expert, start, jnp.arange(EXPERTS, dtype=jnp.int32))
    result = final.astype(jnp.bfloat16)
    return result[0], result[1:]
```

```python
import functools

import jax
import jax.numpy as jnp
from jax import lax
from jax.experimental import pallas as pl
from jax.experimental.pallas import tpu as pltpu
from jax.sharding import PartitionSpec as P

MESH = pl.DeviceIdType.MESH
DISPATCH, ROW_X, ROW_CORE, ROW_DIAG, ACT_X, ACT_CORE, ACT_DIAG, RETURN = range(8)
N_EP, N_TP = 8, 4


def body(tokens, tangents, tangent_mask, expert_ids, gate_fixed, w_up, w_down):
    group, quarter = tokens.shape
    n_ep = lax.axis_size("ep")
    top = expert_ids.shape[1]
    local_experts = w_up.shape[0]
    experts = local_experts * n_ep
    capacity = max(2, min(group, 3 * group * top // (2 * experts)))
    blocks = tangent_mask.shape[2]
    keep = tangent_mask.astype(jnp.bfloat16)
    masked = (tangents.reshape(2, group, blocks, quarter // blocks) * keep[..., None]).reshape(
        2, group, quarter
    )
    stacked = jnp.concatenate([tokens[None], masked], axis=0)
    flat_ids = expert_ids.reshape(-1)
    onehot = (flat_ids[:, None] == jnp.arange(experts, dtype=jnp.int32)[None, :]).astype(jnp.int32)
    rank = jnp.sum((jnp.cumsum(onehot, axis=0) - onehot) * onehot, axis=1)
    dest = flat_ids * capacity + rank
    owner = jnp.full((experts * capacity,), group, jnp.int32)
    owner = owner.at[dest].set(jnp.arange(group * top, dtype=jnp.int32) // top)
    send_cols = jnp.take(stacked, owner, axis=1, mode="fill", fill_value=0)
    send_cols = send_cols.reshape(3, n_ep, local_experts * capacity, quarter)
    arrived = lax.all_to_all(send_cols, "ep", split_axis=1, concat_axis=1, tiled=True)
    routed = arrived.reshape(3, n_ep, local_experts, capacity, quarter)
    weights = w_up
    hidden = jnp.einsum(
        "tsecd,edf->tsecf",
        lax.all_gather(routed, "tp", axis=4, tiled=True),
        weights,
        preferred_element_type=jnp.float32,
    )
    base = hidden[0]
    sig = jax.nn.sigmoid(base)
    slope = sig * (1.0 + base * (1.0 - sig))
    acts = jnp.concatenate([(base * sig)[None], slope[None] * hidden[1:]], axis=0).astype(
        jnp.bfloat16
    )
    out_width = w_down.shape[2]
    weights = w_down
    outs = jnp.einsum(
        "tsecf,efd->tsecd",
        lax.all_gather(acts, "tp", axis=4, tiled=True),
        weights,
        preferred_element_type=jnp.float32,
    ).astype(jnp.bfloat16)
    outs = outs.reshape(3, n_ep, local_experts * capacity, out_width)
    returned = lax.all_to_all(outs, "ep", split_axis=1, concat_axis=1, tiled=True)
    table = returned.reshape(3, experts * capacity, out_width)
    picked = jnp.take(table, dest, axis=1).reshape(3, group, top, out_width)
    gates = gate_fixed.astype(jnp.float32) / 65536.0
    summed = jnp.einsum("tgkd,gk->tgd", picked.astype(jnp.float32), gates).astype(jnp.bfloat16)
    return (summed[0], summed[1:])


def flip(e, position):
    k = position // 2
    dz = (k % 3 + 1) * ((k + 2) // 3)
    bits = (position % 2, dz % 2, dz // 2)
    own = (e % 2, (e // 2) % 2, e // 4)
    mixed = [a + b - 2 * a * b for a, b in zip(own, bits)]
    return mixed[0] + 2 * mixed[1] + 4 * mixed[2]


def fused_kernel(
    cap, tokens, tangents, mask, ids, gates, up_hbm, down_hbm, out, out_tangents,
    stacked, pick, held, rows, acts, results, table, up, down, up_sem, down_sem, send, recv,
):
    e = lax.axis_index("ep")
    p = lax.axis_index("tp")
    group, quarter = tokens.shape
    hidden = up.shape[1]
    x, c = p // 2, p % 2
    p_x = (1 - x) * 2 + c
    p_core = x * 2 + (1 - c)

    def copy(kind, i, src, dst, ep_to, tp_to):
        return pltpu.make_async_remote_copy(
            src_ref=src, dst_ref=dst, send_sem=send.at[kind, i], recv_sem=recv.at[kind, i],
            device_id=(ep_to, tp_to), device_id_type=MESH,
        )

    def dispatch(i):
        return copy(DISPATCH, i, held.at[i], rows.at[p, i], flip(e, i), p)

    def row_x(i):
        return copy(ROW_X, i, rows.at[p, i], rows.at[p, i], e, p_x)

    def row_core(i):
        return copy(ROW_CORE, i, rows.at[p, i], rows.at[p, i], e, p_core)

    def row_diag(i):
        return copy(ROW_DIAG, i, rows.at[p_x, i], rows.at[p_x, i], e, p_core)

    def act_x(i):
        return copy(ACT_X, i, acts.at[p, i], acts.at[p, i], e, p_x)

    def act_core(i):
        return copy(ACT_CORE, i, acts.at[p, i], acts.at[p, i], e, p_core)

    def act_diag(i):
        return copy(ACT_DIAG, i, acts.at[p_x, i], acts.at[p_x, i], e, p_core)

    def give_back(i):
        return copy(RETURN, i, results.at[i], table.at[i], flip(e, i), p)

    load_up = pltpu.make_async_copy(up_hbm.at[0], up, up_sem)
    load_down = pltpu.make_async_copy(down_hbm.at[0], down, down_sem)
    load_up.start()
    load_down.start()

    barrier = pltpu.get_barrier_semaphore()
    for i in range(1, N_EP):
        pl.semaphore_signal(barrier, inc=1, device_id=(flip(e, i), p), device_id_type=MESH)
    for peer in (p_x, p_core):
        pl.semaphore_signal(barrier, inc=1, device_id=(e, peer), device_id_type=MESH)

    stacked[0] = tokens[...]
    blocks = mask.shape[2]
    width = quarter // blocks
    for d in range(2):
        keep = mask[d].astype(jnp.float32)
        for b in range(blocks):
            part = tangents[d, :, b * width:(b + 1) * width].astype(jnp.float32)
            stacked[1 + d, :, b * width:(b + 1) * width] = (part * keep[:, b:b + 1]).astype(jnp.bfloat16)

    named = ids[...]
    relative = jnp.bitwise_xor(named, e)
    dz = relative // 2
    position = jnp.where(dz == 0, 0, (dz + 1) % 3 + 1) * 2 + relative % 2
    lane = lax.broadcasted_iota(jnp.int32, (group, group), 1)
    line = lax.broadcasted_iota(jnp.int32, (group, group), 0)
    first, second = position[:, 0:1] == lane, position[:, 1:2] == lane
    member = jnp.where(first | second, 1.0, 0.0).astype(jnp.bfloat16)
    before = jnp.where(lane < line, 1.0, 0.0).astype(jnp.bfloat16)
    rank = jnp.dot(before, member, preferred_element_type=jnp.float32)
    places = []
    for k, match in enumerate((first, second)):
        own_rank = jnp.sum(jnp.where(match, rank, 0.0), axis=1, keepdims=True).astype(jnp.int32)
        places.append(position[:, k:k + 1] * cap + own_rank)
    slot = lax.broadcasted_iota(jnp.int32, (group, N_EP * cap), 1)
    hits = [place == slot for place in places]
    chosen = jnp.where(hits[0] | hits[1], 1.0, 0.0)
    pick[...] = jnp.transpose(chosen).astype(jnp.bfloat16).reshape(N_EP, cap, group)

    pl.semaphore_wait(barrier, N_EP - 1 + 2)

    def fill(i, target):
        for t in range(3):
            picked = jnp.dot(pick[i], stacked[t], preferred_element_type=jnp.float32)
            target[t * cap:(t + 1) * cap, :] = picked.astype(jnp.bfloat16)

    def send_one(i, carry):
        fill(i, held.at[i])
        dispatch(i).start()
        return carry

    fill(0, rows.at[p, 0])
    lax.fori_loop(1, N_EP, send_one, 0)
    load_up.wait()
    load_down.wait()

    def tick(n, carry):
        @pl.when(n < N_EP)
        def _():
            @pl.when(n > 0)
            def _():
                dispatch(n).wait_recv()
            row_x(n).start()
            row_core(n).start()

        @pl.when((n >= 1) & (n < N_EP + 1))
        def _():
            i = n - 1
            row_x(i).wait_recv()
            row_diag(i).start()
            row_core(i).wait_recv()
            row_diag(i).wait_recv()
            total = jnp.zeros((3 * cap, hidden), jnp.float32)
            for q in range(N_TP):
                total += jnp.dot(
                    rows[q, i], up[q * quarter:(q + 1) * quarter, :], preferred_element_type=jnp.float32
                )
            base = total[:cap]
            sig = jax.nn.sigmoid(base)
            slope = sig * (1.0 + base * (1.0 - sig))
            acts[p, i, :cap, :] = (base * sig).astype(jnp.bfloat16)
            acts[p, i, cap:2 * cap, :] = (slope * total[cap:2 * cap]).astype(jnp.bfloat16)
            acts[p, i, 2 * cap:, :] = (slope * total[2 * cap:]).astype(jnp.bfloat16)
            act_x(i).start()
            act_core(i).start()

        @pl.when(n >= 2)
        def _():
            i = n - 2
            act_x(i).wait_recv()
            act_diag(i).start()
            act_core(i).wait_recv()
            act_diag(i).wait_recv()
            total = jnp.zeros((3 * cap, quarter), jnp.float32)
            for q in range(N_TP):
                total += jnp.dot(
                    acts[q, i], down[q * hidden:(q + 1) * hidden, :], preferred_element_type=jnp.float32
                )
            rounded = total.astype(jnp.bfloat16)

            @pl.when(i > 0)
            def _():
                results[i] = rounded
                give_back(i).start()

            @pl.when(i == 0)
            def _():
                table[0] = rounded

        return carry

    lax.fori_loop(0, N_EP + 2, tick, 0)

    high, low = 0.0, 0.0
    for k in range(2):
        gate = gates[:, k:k + 1]
        high += jnp.where(hits[k], (gate // 256).astype(jnp.float32), 0.0)
        low += jnp.where(hits[k], (gate % 256).astype(jnp.float32), 0.0)
    high, low = high.astype(jnp.bfloat16), low.astype(jnp.bfloat16)

    def drain(i, carry):
        for one in (row_x, row_core, row_diag, act_x, act_core, act_diag):
            one(i).wait_send()

        @pl.when(i > 0)
        def _():
            dispatch(i).wait_send()
            give_back(i).wait_send()
            give_back(i).wait_recv()

        return carry

    lax.fori_loop(0, N_EP, drain, 0)
    for t in range(3):
        back = table[:, t * cap:(t + 1) * cap, :].reshape(N_EP * cap, quarter)
        total = 256.0 * jnp.dot(high, back, preferred_element_type=jnp.float32)
        total += jnp.dot(low, back, preferred_element_type=jnp.float32)
        total = (total * (1.0 / 65536.0)).astype(jnp.bfloat16)
        if t == 0:
            out[...] = total
        else:
            out_tangents[t - 1] = total


def fused(tokens, tangents, tangent_mask, expert_ids, gate_fixed, w_up, w_down):
    group, quarter = tokens.shape
    cap = capacity_of(group, expert_ids.shape[1], N_EP)
    depth, hidden = w_up.shape[1:]
    vmem, hbm = pl.BlockSpec(memory_space=pltpu.VMEM), pl.BlockSpec(memory_space=pl.ANY)
    bf16 = jnp.bfloat16
    return pl.pallas_call(
        functools.partial(fused_kernel, cap),
        out_shape=(
            jax.ShapeDtypeStruct((group, quarter), bf16),
            jax.ShapeDtypeStruct((2, group, quarter), bf16),
        ),
        in_specs=[vmem] * 5 + [hbm] * 2,
        out_specs=(vmem, vmem),
        scratch_shapes=[
            pltpu.VMEM((3, group, quarter), bf16),
            pltpu.VMEM((N_EP, cap, group), bf16),
            pltpu.VMEM((N_EP, 3 * cap, quarter), bf16),
            pltpu.VMEM((N_TP, N_EP, 3 * cap, quarter), bf16),
            pltpu.VMEM((N_TP, N_EP, 3 * cap, hidden), bf16),
            pltpu.VMEM((N_EP, 3 * cap, quarter), bf16),
            pltpu.VMEM((N_EP, 3 * cap, quarter), bf16),
            pltpu.VMEM((depth, hidden), bf16),
            pltpu.VMEM(w_down.shape[1:], bf16),
            pltpu.SemaphoreType.DMA,
            pltpu.SemaphoreType.DMA,
            pltpu.SemaphoreType.DMA((8, N_EP)),
            pltpu.SemaphoreType.DMA((8, N_EP)),
        ],
        compiler_params=pltpu.CompilerParams(
            collective_id=0, has_side_effects=True, vmem_limit_bytes=56 * 1024 * 1024
        ),
    )(tokens, tangents, tangent_mask, expert_ids, gate_fixed, w_up, w_down)


def capacity_of(group, top, experts):
    return max(2, min(group, 3 * group * top // (2 * experts)))


def any_body(*operands):
    tokens, expert_ids, w_up = operands[0], operands[3], operands[5]
    group, quarter = tokens.shape
    fits = (
        lax.axis_size("ep") == N_EP
        and lax.axis_size("tp") == N_TP
        and w_up.shape[0] == 1
        and expert_ids.shape[1] == 2
        and group == 128
        and quarter % 128 == 0
        and capacity_of(group, 2, N_EP) % 16 == 0
    )
    return (fused if fits else body)(*operands)


def solution(mesh):
    placed = (
        P("ep", "tp"),
        P(None, "ep", "tp"),
        P(None, "ep", "tp"),
        P("ep", None),
        P("ep", None),
        P("ep", None, "tp"),
        P("ep", None, "tp"),
    )
    return jax.shard_map(
        any_body,
        mesh=mesh,
        in_specs=placed,
        out_specs=(P("ep", "tp"), P(None, "ep", "tp")),
        check_vma=False,
    )
```

```python
import functools

import jax
import jax.numpy as jnp
from jax import lax
from jax.experimental import pallas as pl
from jax.experimental.pallas import tpu as pltpu
from jax.sharding import PartitionSpec as P

MESH = pl.DeviceIdType.MESH
ROW_X, ROW_CORE, ROW_DIAG, ACT_X, ACT_CORE, ACT_DIAG, NEAR, BACK, DENSE, RELAY, GATHER, PARTIAL = range(12)
N_EP, N_TP = 8, 4


def body(tokens, tangents, tangent_mask, expert_ids, gate_fixed, w_up, w_down):
    group, quarter = tokens.shape
    n_ep = lax.axis_size("ep")
    top = expert_ids.shape[1]
    local_experts = w_up.shape[0]
    experts = local_experts * n_ep
    capacity = max(2, min(group, 3 * group * top // (2 * experts)))
    blocks = tangent_mask.shape[2]
    keep = tangent_mask.astype(jnp.bfloat16)
    masked = (tangents.reshape(2, group, blocks, quarter // blocks) * keep[..., None]).reshape(
        2, group, quarter
    )
    stacked = jnp.concatenate([tokens[None], masked], axis=0)
    flat_ids = expert_ids.reshape(-1)
    onehot = (flat_ids[:, None] == jnp.arange(experts, dtype=jnp.int32)[None, :]).astype(jnp.int32)
    rank = jnp.sum((jnp.cumsum(onehot, axis=0) - onehot) * onehot, axis=1)
    dest = flat_ids * capacity + rank
    owner = jnp.full((experts * capacity,), group, jnp.int32)
    owner = owner.at[dest].set(jnp.arange(group * top, dtype=jnp.int32) // top)
    send_cols = jnp.take(stacked, owner, axis=1, mode="fill", fill_value=0)
    send_cols = send_cols.reshape(3, n_ep, local_experts * capacity, quarter)
    arrived = lax.all_to_all(send_cols, "ep", split_axis=1, concat_axis=1, tiled=True)
    routed = arrived.reshape(3, n_ep, local_experts, capacity, quarter)
    weights = w_up
    hidden = jnp.einsum(
        "tsecd,edf->tsecf",
        lax.all_gather(routed, "tp", axis=4, tiled=True),
        weights,
        preferred_element_type=jnp.float32,
    )
    base = hidden[0]
    sig = jax.nn.sigmoid(base)
    slope = sig * (1.0 + base * (1.0 - sig))
    acts = jnp.concatenate([(base * sig)[None], slope[None] * hidden[1:]], axis=0).astype(
        jnp.bfloat16
    )
    out_width = w_down.shape[2]
    weights = w_down
    outs = jnp.einsum(
        "tsecf,efd->tsecd",
        lax.all_gather(acts, "tp", axis=4, tiled=True),
        weights,
        preferred_element_type=jnp.float32,
    ).astype(jnp.bfloat16)
    outs = outs.reshape(3, n_ep, local_experts * capacity, out_width)
    returned = lax.all_to_all(outs, "ep", split_axis=1, concat_axis=1, tiled=True)
    table = returned.reshape(3, experts * capacity, out_width)
    picked = jnp.take(table, dest, axis=1).reshape(3, group, top, out_width)
    gates = gate_fixed.astype(jnp.float32) / 65536.0
    summed = jnp.einsum("tgkd,gk->tgd", picked.astype(jnp.float32), gates).astype(jnp.bfloat16)
    return (summed[0], summed[1:])


HALF = N_EP // 2
ORDER = (0, 1, 2, 4, 3, 5, 6)


def flip(e, i):
    bits = (e % 2, (e // 2) % 2, e // 4)
    return sum((1 - bit if (i >> n) & 1 else bit) << n for n, bit in enumerate(bits))


def fused_kernel(
    cap, tokens, tangents, mask, ids, gates, up_hbm, down_hbm, out, out_tangents,
    stacked, pick, weights, held, rows, acts, results, table,
    dense, pick_in, weights_in, relayed, far_rows, far_acts, far_results, gathered, partial, partial_in, slopes,
    up, down, up_sem, down_sem, send, recv,
):
    e = lax.axis_index("ep")
    p = lax.axis_index("tp")
    group, quarter = tokens.shape
    hidden = up.shape[1]
    x, c = p // 2, p % 2
    p_x = (1 - x) * 2 + c
    p_core = x * 2 + (1 - c)
    started = []

    def copy(kind, i, src, dst, ep_to, tp_to):
        return pltpu.make_async_remote_copy(
            src_ref=src, dst_ref=dst, send_sem=send.at[kind, i], recv_sem=recv.at[kind, i],
            device_id=(ep_to, tp_to), device_id_type=MESH,
        )

    def start(one):
        one.start()
        started.append(one)

    def spread(kind, u, q, peer):
        buffers, at = (rows, far_rows) if kind <= ROW_DIAG else (acts, far_acts), u
        ref = buffers[0].at[q, u] if u < HALF else buffers[1].at[q, at - HALF]
        return copy(kind, u, ref, ref, e, peer)

    def near(i):
        return copy(NEAR, i, held.at[i], rows.at[p, i], flip(e, i), p)

    def back(i):
        return copy(BACK, i, results.at[i], table.at[i], flip(e, i), p)

    def to_dense(t):
        return copy(DENSE, t, stacked.at[t], dense.at[t], flip(e, HALF), p)

    def to_pick():
        return copy(DENSE, 3, pick.at[pl.ds(HALF, HALF)], pick_in, flip(e, HALF), p)

    def to_weights():
        return copy(DENSE, 4, weights.at[pl.ds(2, 2)], weights_in, flip(e, HALF), p)

    def relay(t, r):
        return copy(RELAY, t * HALF + r, relayed.at[t, r], far_rows.at[p, t, pl.ds(r * cap, cap)], flip(e, r), p)

    def gather(t, r):
        piece = pl.ds(r * cap, cap)
        return copy(GATHER, t * HALF + r, far_results.at[t, piece], gathered.at[t, piece], flip(e, r), p)

    def to_partial(t):
        return copy(PARTIAL, t, partial.at[t], partial_in.at[t], flip(e, HALF), p)

    load_up = pltpu.make_async_copy(up_hbm.at[0], up, up_sem)
    load_down = pltpu.make_async_copy(down_hbm.at[0], down, down_sem)
    load_up.start()
    load_down.start()

    barrier = pltpu.get_barrier_semaphore()
    for i in range(1, HALF + 1):
        pl.semaphore_signal(barrier, inc=1, device_id=(flip(e, i), p), device_id_type=MESH)
    for peer in (p_x, p_core):
        pl.semaphore_signal(barrier, inc=1, device_id=(e, peer), device_id_type=MESH)

    stacked[0] = tokens[...]
    blocks = mask.shape[2]
    width = quarter // blocks
    for d in range(2):
        keep = mask[d].astype(jnp.float32)
        for b in range(blocks):
            part = tangents[d, :, b * width:(b + 1) * width].astype(jnp.float32)
            stacked[1 + d, :, b * width:(b + 1) * width] = (part * keep[:, b:b + 1]).astype(jnp.bfloat16)

    position = jnp.bitwise_xor(ids[...], e)
    lane = lax.broadcasted_iota(jnp.int32, (group, group), 1)
    line = lax.broadcasted_iota(jnp.int32, (group, group), 0)
    first, second = position[:, 0:1] == lane, position[:, 1:2] == lane
    member = jnp.where(first | second, 1.0, 0.0).astype(jnp.bfloat16)
    before = jnp.where(lane < line, 1.0, 0.0).astype(jnp.bfloat16)
    rank = jnp.dot(before, member, preferred_element_type=jnp.float32)
    places = []
    for k, match in enumerate((first, second)):
        own_rank = jnp.sum(jnp.where(match, rank, 0.0), axis=1, keepdims=True).astype(jnp.int32)
        places.append(position[:, k:k + 1] * cap + own_rank)
    slot = lax.broadcasted_iota(jnp.int32, (group, N_EP * cap), 1)
    chosen = jnp.where((places[0] == slot) | (places[1] == slot), 1.0, 0.0)
    pick[...] = jnp.transpose(chosen).astype(jnp.bfloat16).reshape(N_EP, cap, group)

    slot = lax.broadcasted_iota(jnp.int32, (group, HALF * cap), 1)
    for half in range(2):
        high, low = 0.0, 0.0
        for k in range(2):
            gate = gates[:, k:k + 1]
            hit = places[k] == slot + half * HALF * cap
            high += jnp.where(hit, (gate // 256).astype(jnp.float32), 0.0)
            low += jnp.where(hit, (gate % 256).astype(jnp.float32), 0.0)
        weights[2 * half] = high.astype(jnp.bfloat16)
        weights[2 * half + 1] = low.astype(jnp.bfloat16)

    pl.semaphore_wait(barrier, HALF + 2)
    start(to_pick())
    start(to_dense(0))

    def select(one_hot, source):
        return jnp.dot(one_hot, source, preferred_element_type=jnp.float32).astype(jnp.bfloat16)

    def combine(high, low, outs):
        total = 256.0 * jnp.dot(high, outs, preferred_element_type=jnp.float32)
        total += jnp.dot(low, outs, preferred_element_type=jnp.float32)
        return total * (1.0 / 65536.0)

    for t in range(3):
        rows[p, 0, t * cap:(t + 1) * cap, :] = select(pick[0], stacked[t])
    for i in range(1, HALF):
        for t in range(3):
            held[i, t * cap:(t + 1) * cap, :] = select(pick[i], stacked[t])
        start(near(i))
    start(to_dense(1))
    start(to_dense(2))
    start(to_weights())
    load_up.wait()
    load_down.wait()

    def pass_on(t):
        if t == 0:
            to_pick().wait_recv()
        to_dense(t).wait_recv()
        for r in range(1, HALF):
            relayed[t, r] = select(pick_in[r], dense[t])
            start(relay(t, r))
        far_rows[p, t, :cap, :] = select(pick_in[0], dense[t])

    def arrive(u):
        if 0 < u < HALF:
            near(u).wait_recv()
        if u >= HALF:
            for r in range(1, HALF):
                relay(u - HALF, r).wait_recv()
        start(spread(ROW_X, u, p, p_x))
        start(spread(ROW_CORE, u, p, p_core))

    def product(buffers, u, matrix, depth):
        total = 0.0
        for q in range(N_TP):
            left = buffers[0][q, u] if u < HALF else buffers[1][q, u - HALF]
            total += jnp.dot(left, matrix[q * depth:(q + 1) * depth, :], preferred_element_type=jnp.float32)
        return total

    def go_up(u):
        spread(ROW_X, u, p, p_x).wait_recv()
        start(spread(ROW_DIAG, u, p_x, p_core))
        spread(ROW_CORE, u, p, p_core).wait_recv()
        spread(ROW_DIAG, u, p_x, p_core).wait_recv()
        total = product((rows, far_rows), u, up, quarter)
        if u < HALF or u == HALF:
            base = total[:cap] if u < HALF else total
            sig = jax.nn.sigmoid(base)
            slope = sig * (1.0 + base * (1.0 - sig))
            act = (base * sig).astype(jnp.bfloat16)
        if u < HALF:
            acts[p, u, :cap, :] = act
            acts[p, u, cap:2 * cap, :] = (slope * total[cap:2 * cap]).astype(jnp.bfloat16)
            acts[p, u, 2 * cap:, :] = (slope * total[2 * cap:]).astype(jnp.bfloat16)
        elif u == HALF:
            slopes[...] = slope
            far_acts[p, 0] = act
        else:
            far_acts[p, u - HALF] = (slopes[...] * total).astype(jnp.bfloat16)
        start(spread(ACT_X, u, p, p_x))
        start(spread(ACT_CORE, u, p, p_core))

    def go_down(u):
        spread(ACT_X, u, p, p_x).wait_recv()
        start(spread(ACT_DIAG, u, p_x, p_core))
        spread(ACT_CORE, u, p, p_core).wait_recv()
        spread(ACT_DIAG, u, p_x, p_core).wait_recv()
        rounded = product((acts, far_acts), u, down, hidden).astype(jnp.bfloat16)
        if u == 0:
            table[0] = rounded
        elif u < HALF:
            results[u] = rounded
            start(back(u))
        else:
            t = u - HALF
            gathered[t, :cap, :] = rounded[:cap]
            far_results[t, cap:, :] = rounded[cap:]
            for r in range(1, HALF):
                start(gather(t, r))

    def hand_over(t):
        if t == 0:
            to_weights().wait_recv()
        for r in range(1, HALF):
            gather(t, r).wait_recv()
        partial[t] = combine(weights_in[0], weights_in[1], gathered[t]).astype(jnp.bfloat16)
        start(to_partial(t))

    last = len(ORDER)
    for n in range(last + 3):
        if n in (2, 4, 6):
            pass_on(n // 2 - 1)
        if n < last:
            arrive(ORDER[n])
        if 1 <= n < last + 1:
            go_up(ORDER[n - 1])
        if 2 <= n < last + 2:
            go_down(ORDER[n - 2])
        if n >= 3 and ORDER[n - 3] >= HALF:
            hand_over(ORDER[n - 3] - HALF)

    for i in range(1, HALF):
        back(i).wait_recv()
    for t in range(3):
        outs = table[:, t * cap:(t + 1) * cap, :].reshape(HALF * cap, quarter)
        total = combine(weights[0], weights[1], outs)
        to_partial(t).wait_recv()
        total = (total + partial_in[t].astype(jnp.float32)).astype(jnp.bfloat16)
        if t == 0:
            out[...] = total
        else:
            out_tangents[t - 1] = total
    for one in started:
        one.wait_send()


def fused(tokens, tangents, tangent_mask, expert_ids, gate_fixed, w_up, w_down):
    group, quarter = tokens.shape
    cap = capacity_of(group, expert_ids.shape[1], N_EP)
    depth, hidden = w_up.shape[1:]
    vmem, hbm = pl.BlockSpec(memory_space=pltpu.VMEM), pl.BlockSpec(memory_space=pl.ANY)
    bf16 = jnp.bfloat16
    return pl.pallas_call(
        functools.partial(fused_kernel, cap),
        out_shape=(
            jax.ShapeDtypeStruct((group, quarter), bf16),
            jax.ShapeDtypeStruct((2, group, quarter), bf16),
        ),
        in_specs=[vmem] * 5 + [hbm] * 2,
        out_specs=(vmem, vmem),
        scratch_shapes=[
            pltpu.VMEM((3, group, quarter), bf16),
            pltpu.VMEM((N_EP, cap, group), bf16),
            pltpu.VMEM((4, group, HALF * cap), bf16),
            pltpu.VMEM((HALF, 3 * cap, quarter), bf16),
            pltpu.VMEM((N_TP, HALF, 3 * cap, quarter), bf16),
            pltpu.VMEM((N_TP, HALF, 3 * cap, hidden), bf16),
            pltpu.VMEM((HALF, 3 * cap, quarter), bf16),
            pltpu.VMEM((HALF, 3 * cap, quarter), bf16),
            pltpu.VMEM((3, group, quarter), bf16),
            pltpu.VMEM((HALF, cap, group), bf16),
            pltpu.VMEM((2, group, HALF * cap), bf16),
            pltpu.VMEM((3, HALF, cap, quarter), bf16),
            pltpu.VMEM((N_TP, 3, HALF * cap, quarter), bf16),
            pltpu.VMEM((N_TP, 3, HALF * cap, hidden), bf16),
            pltpu.VMEM((3, HALF * cap, quarter), bf16),
            pltpu.VMEM((3, HALF * cap, quarter), bf16),
            pltpu.VMEM((3, group, quarter), bf16),
            pltpu.VMEM((3, group, quarter), bf16),
            pltpu.VMEM((HALF * cap, hidden), jnp.float32),
            pltpu.VMEM((depth, hidden), bf16),
            pltpu.VMEM(w_down.shape[1:], bf16),
            pltpu.SemaphoreType.DMA,
            pltpu.SemaphoreType.DMA,
            pltpu.SemaphoreType.DMA((12, 3 * HALF)),
            pltpu.SemaphoreType.DMA((12, 3 * HALF)),
        ],
        compiler_params=pltpu.CompilerParams(
            collective_id=0, has_side_effects=True, vmem_limit_bytes=56 * 1024 * 1024
        ),
    )(tokens, tangents, tangent_mask, expert_ids, gate_fixed, w_up, w_down)


def capacity_of(group, top, experts):
    return max(2, min(group, 3 * group * top // (2 * experts)))


def any_body(*operands):
    tokens, expert_ids, w_up = operands[0], operands[3], operands[5]
    group, quarter = tokens.shape
    fits = (
        lax.axis_size("ep") == N_EP
        and lax.axis_size("tp") == N_TP
        and w_up.shape[0] == 1
        and expert_ids.shape[1] == 2
        and group == 128
        and quarter % 128 == 0
        and capacity_of(group, 2, N_EP) % 16 == 0
    )
    return (fused if fits else body)(*operands)


def solution(mesh):
    placed = (
        P("ep", "tp"),
        P(None, "ep", "tp"),
        P(None, "ep", "tp"),
        P("ep", None),
        P("ep", None),
        P("ep", None, "tp"),
        P("ep", None, "tp"),
    )
    return jax.shard_map(
        any_body,
        mesh=mesh,
        in_specs=placed,
        out_specs=(P("ep", "tp"), P(None, "ep", "tp")),
        check_vma=False,
    )
```

```python
import functools

import jax
import jax.numpy as jnp
from jax import lax
from jax.experimental import pallas as pl
from jax.experimental.pallas import tpu as pltpu
from jax.sharding import PartitionSpec as P

MESH = pl.DeviceIdType.MESH
DISPATCH, ROW_X, ROW_CORE, ROW_DIAG, ACT_X, ACT_CORE, ACT_DIAG, RETURN = range(8)
N_EP, N_TP = 8, 4


def body(tokens, tangents, tangent_mask, expert_ids, gate_fixed, w_up, w_down):
    group, quarter = tokens.shape
    n_ep = lax.axis_size("ep")
    top = expert_ids.shape[1]
    local_experts = w_up.shape[0]
    experts = local_experts * n_ep
    capacity = max(2, min(group, 3 * group * top // (2 * experts)))
    blocks = tangent_mask.shape[2]
    keep = tangent_mask.astype(jnp.bfloat16)
    masked = (tangents.reshape(2, group, blocks, quarter // blocks) * keep[..., None]).reshape(
        2, group, quarter
    )
    stacked = jnp.concatenate([tokens[None], masked], axis=0)
    flat_ids = expert_ids.reshape(-1)
    onehot = (flat_ids[:, None] == jnp.arange(experts, dtype=jnp.int32)[None, :]).astype(jnp.int32)
    rank = jnp.sum((jnp.cumsum(onehot, axis=0) - onehot) * onehot, axis=1)
    dest = flat_ids * capacity + rank
    owner = jnp.full((experts * capacity,), group, jnp.int32)
    owner = owner.at[dest].set(jnp.arange(group * top, dtype=jnp.int32) // top)
    send_cols = jnp.take(stacked, owner, axis=1, mode="fill", fill_value=0)
    send_cols = send_cols.reshape(3, n_ep, local_experts * capacity, quarter)
    arrived = lax.all_to_all(send_cols, "ep", split_axis=1, concat_axis=1, tiled=True)
    routed = arrived.reshape(3, n_ep, local_experts, capacity, quarter)
    weights = w_up
    hidden = jnp.einsum(
        "tsecd,edf->tsecf",
        lax.all_gather(routed, "tp", axis=4, tiled=True),
        weights,
        preferred_element_type=jnp.float32,
    )
    base = hidden[0]
    sig = jax.nn.sigmoid(base)
    slope = sig * (1.0 + base * (1.0 - sig))
    acts = jnp.concatenate([(base * sig)[None], slope[None] * hidden[1:]], axis=0).astype(
        jnp.bfloat16
    )
    out_width = w_down.shape[2]
    weights = w_down
    outs = jnp.einsum(
        "tsecf,efd->tsecd",
        lax.all_gather(acts, "tp", axis=4, tiled=True),
        weights,
        preferred_element_type=jnp.float32,
    ).astype(jnp.bfloat16)
    outs = outs.reshape(3, n_ep, local_experts * capacity, out_width)
    returned = lax.all_to_all(outs, "ep", split_axis=1, concat_axis=1, tiled=True)
    table = returned.reshape(3, experts * capacity, out_width)
    picked = jnp.take(table, dest, axis=1).reshape(3, group, top, out_width)
    gates = gate_fixed.astype(jnp.float32) / 65536.0
    summed = jnp.einsum("tgkd,gk->tgd", picked.astype(jnp.float32), gates).astype(jnp.bfloat16)
    return (summed[0], summed[1:])


def flip(e, position):
    k = position // 2
    dz = k
    bits = (position % 2, dz % 2, dz // 2)
    own = (e % 2, (e // 2) % 2, e // 4)
    mixed = [a + b - 2 * a * b for a, b in zip(own, bits)]
    return mixed[0] + 2 * mixed[1] + 4 * mixed[2]


def fused_kernel(
    cap, tokens, tangents, mask, ids, gates, up_hbm, down_hbm, out, out_tangents,
    stacked, pick, held, rows, acts, results, table, early, lines, up, down, up_sem, down_sem, send, recv,
):
    e = lax.axis_index("ep")
    p = lax.axis_index("tp")
    group, quarter = tokens.shape
    hidden = up.shape[1]
    x, c = p // 2, p % 2
    p_x = (1 - x) * 2 + c
    p_core = x * 2 + (1 - c)

    def copy(kind, i, src, dst, ep_to, tp_to):
        return pltpu.make_async_remote_copy(
            src_ref=src, dst_ref=dst, send_sem=send.at[kind, i], recv_sem=recv.at[kind, i],
            device_id=(ep_to, tp_to), device_id_type=MESH,
        )

    def dispatch(i):
        return copy(DISPATCH, i, held.at[i], rows.at[p, i], flip(e, i), p)

    def row_x(i):
        return copy(ROW_X, i, rows.at[p, i], rows.at[p, i], e, p_x)

    def row_core(i):
        return copy(ROW_CORE, i, rows.at[p, i], rows.at[p, i], e, p_core)

    def row_diag(i):
        return copy(ROW_DIAG, i, rows.at[p_x, i], rows.at[p_x, i], e, p_core)

    def act_x(i):
        return copy(ACT_X, i, acts.at[p, i], acts.at[p, i], e, p_x)

    def act_core(i):
        return copy(ACT_CORE, i, acts.at[p, i], acts.at[p, i], e, p_core)

    def act_diag(i):
        return copy(ACT_DIAG, i, acts.at[p_x, i], acts.at[p_x, i], e, p_core)

    def give_back(i):
        return copy(RETURN, i, results.at[i], table.at[i], flip(e, i), p)

    load_up = pltpu.make_async_copy(up_hbm.at[0], up, up_sem)
    load_down = pltpu.make_async_copy(down_hbm.at[0], down, down_sem)
    load_up.start()
    load_down.start()

    barrier = pltpu.get_barrier_semaphore()
    for i in range(1, N_EP):
        pl.semaphore_signal(barrier, inc=1, device_id=(flip(e, i), p), device_id_type=MESH)
    for peer in (p_x, p_core):
        pl.semaphore_signal(barrier, inc=1, device_id=(e, peer), device_id_type=MESH)

    lines[...] = jnp.zeros_like(lines)
    lines[0:2, :] = ids[...]
    lines[2:4, :] = gates[...]
    for b in range(mask.shape[0]):
        lines[4 + 2 * b:6 + 2 * b, :] = mask[b]
    by_token = jnp.transpose(lines[...].astype(jnp.float32))
    small = by_token.astype(jnp.int32)

    stacked[0] = tokens[...]
    blocks = mask.shape[0]
    width = quarter // blocks
    for d in range(2):
        keep = by_token[:, 4:4 + 2 * blocks]
        for b in range(blocks):
            part = tangents[d, :, b * width:(b + 1) * width].astype(jnp.float32)
            stacked[1 + d, :, b * width:(b + 1) * width] = (part * keep[:, 2 * b + d:2 * b + d + 1]).astype(jnp.bfloat16)

    position = jnp.bitwise_xor(small[:, 0:2], e)
    lane = lax.broadcasted_iota(jnp.int32, (group, group), 1)
    line = lax.broadcasted_iota(jnp.int32, (group, group), 0)
    first, second = position[:, 0:1] == lane, position[:, 1:2] == lane
    member = jnp.where(first | second, 1.0, 0.0).astype(jnp.bfloat16)
    before = jnp.where(lane < line, 1.0, 0.0).astype(jnp.bfloat16)
    rank = jnp.dot(before, member, preferred_element_type=jnp.float32)
    places = []
    for k, match in enumerate((first, second)):
        own_rank = jnp.sum(jnp.where(match, rank, 0.0), axis=1, keepdims=True).astype(jnp.int32)
        places.append(position[:, k:k + 1] * cap + own_rank)
    slot = lax.broadcasted_iota(jnp.int32, (group, N_EP * cap), 1)
    hits = [place == slot for place in places]
    chosen = jnp.where(hits[0] | hits[1], 1.0, 0.0)
    pick[...] = jnp.transpose(chosen).astype(jnp.bfloat16).reshape(N_EP, cap, group)

    pl.semaphore_wait(barrier, N_EP - 1 + 2)

    def fill(i, target):
        for t in range(3):
            picked = jnp.dot(pick[i], stacked[t], preferred_element_type=jnp.float32)
            target[t * cap:(t + 1) * cap, :] = picked.astype(jnp.bfloat16)

    def send_one(i, carry):
        fill(i, held.at[i])
        dispatch(i).start()
        return carry

    fill(0, rows.at[p, 0])
    lax.fori_loop(1, N_EP, send_one, 0)
    load_up.wait()
    load_down.wait()

    def tick(n, carry):
        @pl.when(n < N_EP)
        def _():
            @pl.when(n > 0)
            def _():
                dispatch(n).wait_recv()
            row_x(n).start()
            row_core(n).start()

        @pl.when((n >= 1) & (n < N_EP + 1))
        def _():
            i = n - 1
            row_x(i).wait_recv()
            row_diag(i).start()
            row_core(i).wait_recv()
            row_diag(i).wait_recv()
            total = jnp.zeros((3 * cap, hidden), jnp.float32)
            for q in range(N_TP):
                total += jnp.dot(
                    rows[q, i], up[q * quarter:(q + 1) * quarter, :], preferred_element_type=jnp.float32
                )
            base = total[:cap]
            sig = jax.nn.sigmoid(base)
            slope = sig * (1.0 + base * (1.0 - sig))
            acts[p, i, :cap, :] = (base * sig).astype(jnp.bfloat16)
            acts[p, i, cap:2 * cap, :] = (slope * total[cap:2 * cap]).astype(jnp.bfloat16)
            acts[p, i, 2 * cap:, :] = (slope * total[2 * cap:]).astype(jnp.bfloat16)
            act_x(i).start()
            act_core(i).start()

        @pl.when(n >= 2)
        def _():
            i = n - 2
            act_x(i).wait_recv()
            act_diag(i).start()
            act_core(i).wait_recv()
            act_diag(i).wait_recv()
            total = jnp.zeros((3 * cap, quarter), jnp.float32)
            for q in range(N_TP):
                total += jnp.dot(
                    acts[q, i], down[q * hidden:(q + 1) * hidden, :], preferred_element_type=jnp.float32
                )
            rounded = total.astype(jnp.bfloat16)

            @pl.when(i > 0)
            def _():
                results[i] = rounded
                give_back(i).start()

            @pl.when(i == 0)
            def _():
                table[0] = rounded

        return carry

    lax.fori_loop(0, N_EP + 2, tick, 0)

    def combine(t, lo_at, hi_at):
        columns = lax.broadcasted_iota(jnp.int32, (group, (hi_at - lo_at) * cap), 1) + lo_at * cap
        high, low = 0.0, 0.0
        for k in range(2):
            gate = small[:, 2 + k:3 + k]
            hit = places[k] == columns
            high += jnp.where(hit, (gate // 256).astype(jnp.float32), 0.0)
            low += jnp.where(hit, (gate % 256).astype(jnp.float32), 0.0)
        back = table[lo_at:hi_at, t * cap:(t + 1) * cap, :].reshape((hi_at - lo_at) * cap, quarter)
        total = 256.0 * jnp.dot(high.astype(jnp.bfloat16), back, preferred_element_type=jnp.float32)
        return total + jnp.dot(low.astype(jnp.bfloat16), back, preferred_element_type=jnp.float32)

    def returned(i, carry):
        give_back(i).wait_recv()
        return carry

    def drain(i, carry):
        for one in (row_x, row_core, row_diag, act_x, act_core, act_diag):
            one(i).wait_send()

        @pl.when(i > 0)
        def _():
            dispatch(i).wait_send()

        return carry

    lax.fori_loop(1, N_EP - 2, returned, 0)
    for t in range(3):
        early[t] = combine(t, 0, N_EP - 2)
    lax.fori_loop(0, N_EP, drain, 0)
    lax.fori_loop(N_EP - 2, N_EP, returned, 0)
    for t in range(3):
        total = early[t] + combine(t, N_EP - 2, N_EP)
        total = (total * (1.0 / 65536.0)).astype(jnp.bfloat16)
        if t == 0:
            out[...] = total
        else:
            out_tangents[t - 1] = total

    def sent(i, carry):
        give_back(i).wait_send()
        return carry

    lax.fori_loop(1, N_EP, sent, 0)


def fused(tokens, tangents, tangent_mask, expert_ids, gate_fixed, w_up, w_down):
    group, quarter = tokens.shape
    cap = capacity_of(group, expert_ids.shape[1], N_EP)
    depth, hidden = w_up.shape[1:]
    vmem, hbm = pl.BlockSpec(memory_space=pltpu.VMEM), pl.BlockSpec(memory_space=pl.ANY)
    bf16 = jnp.bfloat16
    return pl.pallas_call(
        functools.partial(fused_kernel, cap),
        out_shape=(
            jax.ShapeDtypeStruct((group, quarter), bf16),
            jax.ShapeDtypeStruct((2, group, quarter), bf16),
        ),
        in_specs=[vmem] * 5 + [hbm] * 2,
        out_specs=(vmem, vmem),
        scratch_shapes=[
            pltpu.VMEM((3, group, quarter), bf16),
            pltpu.VMEM((N_EP, cap, group), bf16),
            pltpu.VMEM((N_EP, 3 * cap, quarter), bf16),
            pltpu.VMEM((N_TP, N_EP, 3 * cap, quarter), bf16),
            pltpu.VMEM((N_TP, N_EP, 3 * cap, hidden), bf16),
            pltpu.VMEM((N_EP, 3 * cap, quarter), bf16),
            pltpu.VMEM((N_EP, 3 * cap, quarter), bf16),
            pltpu.VMEM((3, group, quarter), jnp.float32),
            pltpu.VMEM((group, group), jnp.int32),
            pltpu.VMEM((depth, hidden), bf16),
            pltpu.VMEM(w_down.shape[1:], bf16),
            pltpu.SemaphoreType.DMA,
            pltpu.SemaphoreType.DMA,
            pltpu.SemaphoreType.DMA((8, N_EP)),
            pltpu.SemaphoreType.DMA((8, N_EP)),
        ],
        compiler_params=pltpu.CompilerParams(
            collective_id=0, has_side_effects=True, vmem_limit_bytes=56 * 1024 * 1024
        ),
    )(tokens, tangents, tangent_mask.transpose(2, 0, 1), expert_ids.T, gate_fixed.T, w_up, w_down)


def capacity_of(group, top, experts):
    return max(2, min(group, 3 * group * top // (2 * experts)))


def any_body(*operands):
    tokens, expert_ids, w_up = operands[0], operands[3], operands[5]
    group, quarter = tokens.shape
    fits = (
        lax.axis_size("ep") == N_EP
        and lax.axis_size("tp") == N_TP
        and w_up.shape[0] == 1
        and expert_ids.shape[1] == 2
        and group == 128
        and quarter % 128 == 0
        and 4 + 2 * operands[2].shape[2] <= group
        and capacity_of(group, 2, N_EP) % 16 == 0
    )
    return (fused if fits else body)(*operands)


def solution(mesh):
    placed = (
        P("ep", "tp"),
        P(None, "ep", "tp"),
        P(None, "ep", "tp"),
        P("ep", None),
        P("ep", None),
        P("ep", None, "tp"),
        P("ep", None, "tp"),
    )
    return jax.shard_map(
        any_body,
        mesh=mesh,
        in_specs=placed,
        out_specs=(P("ep", "tp"), P(None, "ep", "tp")),
        check_vma=False,
    )
```
